32 devices in a mesh: row: 4 (over y, x), col: 8 (over z, core).
Axes of the slice: x: 2, y: 2, z: 4, core: 2. Of those that a mesh axis runs over, the one named last changes fastest.
Arguments:
- replay_pool: bfloat16 [4096, 512], P('row'), may hold values from -6 to 6
- sample_ids: int32 [4, 1024], P('row'), may hold values from 0 to 1023, each once within a row
- rotation_bins: int32 [4096], P('row'), may hold values from 0 to 15
Outputs:
- factored: float32 [4096, 4096], P('row', 'col')
The draws below stay inside these ranges and needn't reach their ends.
Inputs may be any that keep to these rules, and one draw needn't show every extreme that they name: Each row of sample_ids is a permutation of 0 to 1023.
All inputs are finite; a program needn't handle non-finite values.
Results may differ from the reference program's by a relative error of at most 0.0003.
Values may be sent and summed in bfloat16 or wider, within the bound.
No kernel may reach another device: no remote copies, remote signals or barrier semaphores. Data moves between devices by JAX's collectives and lax.ppermute only.
A program may use at most 128 MiB of HBM per device.

```python
import jax
import jax.numpy as jnp
from jax import lax

F = 512
ROTS = 16
ROWS_DEV = 1024
CHANNELS = 32
ROWGRID = 4
COLGRID = 8
N = 4096
NB_R = 256
NB_C = 128
PANEL = 1024


latent_rank = 8


noise_level = 0.5


def draw_replay_pool(key, part):
    keys = jax.random.split(jax.random.fold_in(key, 7), 5)
    latent = jax.random.normal(keys[0], (N, latent_rank), jnp.float32)
    noise = jax.random.normal(keys[1], (N, F), jnp.float32)
    amplitude = jax.random.normal(keys[3], (latent_rank, 1, CHANNELS), jnp.float32)
    phase = jax.random.uniform(keys[4], (latent_rank, 1, CHANNELS), jnp.float32, 0.0, 2.0 * jnp.pi)
    bins = jnp.arange(ROTS, dtype=jnp.float32)[None, :, None]
    freqs = jnp.arange(latent_rank, dtype=jnp.float32)[:, None, None]
    pattern = 1.4142135 * amplitude * jnp.cos(2.0 * jnp.pi * freqs * bins / ROTS + phase)
    pattern = pattern.reshape(latent_rank, F)
    signal = jnp.zeros((N, F), jnp.float32)
    for factor in range(latent_rank):
        signal = signal + latent[:, factor:factor + 1] * pattern[factor][None, :]
    signal = signal / jnp.sqrt(jnp.float32(latent_rank))
    values = signal + noise_level * noise
    return jnp.clip(values, -6.0, 6.0).astype(jnp.bfloat16)


def plant(values, rng, smallest, high):
    spot = [jax.random.randint(jax.random.fold_in(rng, axis), (), 0, length) for axis, length in enumerate(values.shape)]
    main_axis = values.shape.index(max(values.shape))
    neighbour = spot[:main_axis] + [(spot[main_axis] + 1) % values.shape[main_axis]] + spot[main_axis + 1:]
    return values.at[tuple(spot)].set(smallest).at[tuple(neighbour)].set(high)


def setup_inputs(seed: int = 0) -> dict:
    key_list = jax.random.split(jax.random.key(seed), 4)
    return {
        "replay_pool": draw_replay_pool(jax.random.fold_in(key_list[3], 71), 0),
        "sample_ids": jax.vmap(lambda own: jax.random.permutation(own, ROWS_DEV))(jax.random.split(key_list[1], ROWGRID)).reshape((ROWGRID, ROWS_DEV)).astype(jnp.int32),
        "rotation_bins": plant(jax.random.randint(key_list[2], (N,), 0, ROTS), jax.random.fold_in(key_list[2], 1), 0, ROTS - 1).astype(jnp.int32),
    }


sharpness = 2.0
ridge_weight = 0.1
highest = lax.Precision.HIGHEST

def action_weight(row_rot, col_rot):
    bin_gap = (row_rot[:, None] - col_rot[None, :]).astype(jnp.float32)
    return jnp.exp(sharpness * (jnp.cos(bin_gap * (2.0 * jnp.pi / ROTS)) - 1.0))

def orbit_kernel(row_feats, row_rot, col_feats, col_rot):
    rows_wide = row_feats.astype(jnp.float32)
    cols_wide = col_feats.astype(jnp.float32)
    row_norms = jnp.sum(rows_wide * rows_wide, axis=1)
    col_norms = jnp.sum(cols_wide * cols_wide, axis=1)
    col_binned = cols_wide.reshape(cols_wide.shape[0], ROTS, CHANNELS)

    def one_rotation(summed, rotation):
        rolled = jnp.roll(col_binned, rotation, axis=1).reshape(cols_wide.shape[0], F)
        products = jnp.dot(rows_wide, rolled.T, precision=highest)
        distance = row_norms[:, None] + col_norms[None, :] - 2.0 * products
        return (summed + jnp.exp(-distance / F), None)
    start = jnp.zeros((rows_wide.shape[0], cols_wide.shape[0]), jnp.float32)
    summed, _ = lax.scan(one_rotation, start, jnp.arange(ROTS, dtype=jnp.int32))
    return action_weight(row_rot, col_rot) * summed / ROTS

def reference(replay_pool, sample_ids, rotation_bins):
    offsets = (jnp.arange(ROWGRID, dtype=jnp.int32) * ROWS_DEV)[:, None]
    features = replay_pool[(sample_ids + offsets).reshape(N)]
    kernel_full = orbit_kernel(features, rotation_bins, features, rotation_bins)
    kernel_full = kernel_full + ridge_weight * jnp.eye(N, dtype=jnp.float32)
    diag_factor = jnp.linalg.cholesky(kernel_full[:PANEL, :PANEL])
    panel = jax.scipy.linalg.solve_triangular(diag_factor, kernel_full[:, :PANEL].T, lower=True).T
    trailing = kernel_full[:, PANEL:] - jnp.dot(panel, panel[PANEL:].T, precision=highest)
    updated = jnp.concatenate([panel, trailing], axis=1)
    by_rows = updated.reshape(ROWGRID, ROWGRID, NB_R, N).transpose(1, 0, 2, 3).reshape(N, N)
    return by_rows.reshape(N, ROWGRID, COLGRID, NB_C).transpose(0, 2, 1, 3).reshape(N, N)
```

```python
import functools

import jax
import jax.numpy as jnp
import numpy as np
from jax import lax
from jax.experimental import pallas as pl
from jax.experimental.pallas import tpu as pltpu
from jax.sharding import PartitionSpec as P

ROTS = 16
SHARPNESS = 2.0
RIDGE = 0.1
BIG = 256
SMALL = 128
F32, BF16 = jnp.float32, jnp.bfloat16


def split(x):
    hi = x.astype(BF16)
    return hi, (x - hi.astype(F32)).astype(BF16)


def dot_nt(a, b):
    return lax.dot_general(a, b, (((1,), (1,)), ((), ())), preferred_element_type=F32)


def dot_nn(a, b):
    return jnp.dot(a, b, preferred_element_type=F32)


def dot3(dot, ah, al, bh, bl):
    return dot(ah, bh) + (dot(ah, bl) + dot(al, bh))


def gauss_jordan(rows):
    groups = len(rows)
    shape = (8, SMALL)
    sub = lax.broadcasted_iota(jnp.int32, shape, 0)
    lane = lax.broadcasted_iota(jnp.int32, shape, 1)
    left = list(rows)
    right = [jnp.where(sub + 8 * g == lane, 1.0, 0.0).astype(F32) for g in range(groups)]
    out = []
    for g in range(groups):
        a, b = left[g], right[g]
        cols = [jnp.broadcast_to(a[:, 8 * g + k : 8 * g + k + 1], shape) for k in range(8)]
        kept = jnp.zeros(shape, F32)
        for k in range(8):
            pivot = jnp.broadcast_to(cols[k][k : k + 1, :], shape)
            inv = 1.0 / pivot
            mult = jnp.where(sub == k, 1.0 - inv, cols[k] * inv)
            arow = jnp.broadcast_to(a[k : k + 1, :], shape)
            brow = jnp.broadcast_to(b[k : k + 1, :], shape)
            kept = jnp.where(sub == k, brow * lax.rsqrt(pivot), kept)
            a = a - mult * arow
            b = b - mult * brow
            for j in range(k + 1, 8):
                cols[j] = cols[j] - mult * jnp.broadcast_to(cols[j][k : k + 1, :], shape)
        out.append(kept)
        for i in range(g + 1, groups):
            suma = sumb = None
            for k in range(8):
                c = jnp.broadcast_to(left[i][:, 8 * g + k : 8 * g + k + 1], shape)
                ta = c * jnp.broadcast_to(a[k : k + 1, :], shape)
                tb = c * jnp.broadcast_to(b[k : k + 1, :], shape)
                suma, sumb = (ta, tb) if suma is None else (suma + ta, sumb + tb)
            left[i] = left[i] - suma
            right[i] = right[i] - sumb
    return out


def mega_kernel(dims, pq_ref, x_ref, lt_ref, ct_ref, xi_ref, li_ref, ci_ref, *refs):
    lead, other, block_rows, rows_other, tile_other, width = dims
    trail_out, *refs = refs
    if width is None:
        lead_out, *refs = refs
    s_ref, ph_ref, pl_ref, d_ref, x32_ref, ln_ref, cn_ref = refs
    feat = x_ref.shape[1]
    chan = feat // ROTS
    nbig = lead // BIG
    cols_pad = ct_ref.shape[1]

    def evaluate(row0, tm, t_ref, info_ref, norm_ref, col0, tn):
        a = x_ref[pl.ds(row0, tm), :]
        acc = None
        for s in range(ROTS):
            w = t_ref[feat - chan * s : 2 * feat - chan * s, pl.ds(col0, tn)]
            e = jnp.exp(dot_nn(a, w))
            acc = e if acc is None else acc + e
        af = a.astype(F32)
        rn = jnp.sum(af * af, axis=1, keepdims=True) * (1.0 / feat)
        info = xi_ref[pl.ds(row0, tm), :]
        rc, rs, rg = info[:, 0:1], info[:, 1:2], info[:, 2:3]
        cc, cs, cg = (info_ref[k : k + 1, pl.ds(col0, tn)] for k in range(3))
        cn = norm_ref[0:1, pl.ds(col0, tn)]
        arg = (2.0 * rc) * cc + (2.0 * rs) * cs - (rn + SHARPNESS) - cn
        value = acc * jnp.exp(arg) * (1.0 / ROTS)
        return value + jnp.where(rg == cg, RIDGE, 0.0).astype(F32)

    def al(v, m):
        return pl.multiple_of(v, m)

    for t_ref, norm_ref in ((lt_ref, ln_ref), (ct_ref, cn_ref)):
        t = t_ref[0:feat, :].astype(F32)
        norm_ref[0:1, :] = jnp.sum(t * t, axis=0, keepdims=True) * (256.0 * 256.0 / feat)

    def lead_col(j, _):
        def lead_row(i, _):
            r0, c0 = al(i * BIG, BIG), al(j * BIG, BIG)
            s_ref[pl.ds(r0, BIG), pl.ds(c0, BIG)] = evaluate(r0, BIG, lt_ref, li_ref, ln_ref, c0, BIG)
            return 0
        lax.fori_loop(j, nbig, lead_row, 0)
        def upper_row(i, _):
            r0, c0 = al(i * BIG, BIG), al(j * BIG, BIG)
            s_ref[pl.ds(r0, BIG), pl.ds(c0, BIG)] = jnp.zeros((BIG, BIG), F32)
            ph_ref[pl.ds(r0, BIG), pl.ds(c0, BIG)] = jnp.zeros((BIG, BIG), BF16)
            pl_ref[pl.ds(r0, BIG), pl.ds(c0, BIG)] = jnp.zeros((BIG, BIG), BF16)
            return 0
        lax.fori_loop(0, j, upper_row, 0)
        def other_row(i, _):
            r0, c0 = al(lead + i * tile_other, SMALL), al(j * BIG, BIG)
            s_ref[pl.ds(r0, tile_other), pl.ds(c0, BIG)] = evaluate(r0, tile_other, lt_ref, li_ref, ln_ref, c0, BIG)
            return 0
        lax.fori_loop(0, other // tile_other, other_row, 0)
        return 0
    lax.fori_loop(0, nbig, lead_col, 0)

    def invert(r0):
        rows = [d_ref[r0 + 8 * g : r0 + 8 * g + 8, r0 : r0 + SMALL] for g in range(SMALL // 8)]
        for g, v in enumerate(gauss_jordan(rows)):
            x32_ref[r0 + 8 * g : r0 + 8 * g + 8, r0 : r0 + SMALL] = v

    def big_step(j, _):
        c0 = al(j * BIG, BIG)
        cj = pl.ds(c0, BIG)
        d_ref[...] = s_ref[cj, cj]
        invert(0)
        x11 = split(x32_ref[0:SMALL, 0:SMALL])
        l21 = dot3(dot_nt, *split(d_ref[SMALL:, 0:SMALL]), *x11)
        l21s = split(l21)
        d_ref[SMALL:, SMALL:] = d_ref[SMALL:, SMALL:] - dot3(dot_nt, *l21s, *l21s)
        invert(SMALL)
        x22 = split(x32_ref[SMALL:, SMALL:])
        mid = split(dot3(dot_nn, *l21s, *x11))
        x32_ref[SMALL:, 0:SMALL] = -dot3(dot_nn, *x22, *mid)
        x32_ref[0:SMALL, SMALL:] = jnp.zeros((SMALL, SMALL), F32)
        xh, xl = split(x32_ref[...])

        def solve(r0, tm, mask):
            v = dot3(dot_nt, *split(s_ref[pl.ds(r0, tm), cj]), xh, xl)
            if mask:
                keep = lax.broadcasted_iota(jnp.int32, v.shape, 0) >= lax.broadcasted_iota(jnp.int32, v.shape, 1)
                v = jnp.where(keep, v, 0.0)
            s_ref[pl.ds(r0, tm), cj] = v
            h, l = split(v)
            ph_ref[pl.ds(r0, tm), cj] = h
            pl_ref[pl.ds(r0, tm), cj] = l

        solve(c0, BIG, True)
        def lead_solve(i, _):
            solve(al(i * BIG, BIG), BIG, False)
            return 0
        lax.fori_loop(j + 1, nbig, lead_solve, 0)
        def other_solve(i, _):
            solve(al(lead + i * tile_other, SMALL), tile_other, False)
            return 0
        lax.fori_loop(0, other // tile_other, other_solve, 0)

        def update(r0, tm, k0):
            kj = pl.ds(k0, BIG)
            rows = pl.ds(r0, tm)
            s_ref[rows, kj] = s_ref[rows, kj] - dot3(
                dot_nt, ph_ref[rows, cj], pl_ref[rows, cj], ph_ref[kj, cj], pl_ref[kj, cj])

        def update_col(k, _):
            k0 = al(k * BIG, BIG)
            def lead_update(i, _):
                update(al(i * BIG, BIG), BIG, k0)
                return 0
            lax.fori_loop(k, nbig, lead_update, 0)
            def other_update(i, _):
                update(al(lead + i * tile_other, SMALL), tile_other, k0)
                return 0
            lax.fori_loop(0, other // tile_other, other_update, 0)
            return 0
        lax.fori_loop(j + 1, nbig, update_col, 0)
        return 0
    lax.fori_loop(0, nbig, big_step, 0)

    first = al(pq_ref[0] * block_rows, block_rows)
    cols0 = lead + rows_other
    groups = 1 + rows_other // block_rows

    def trailing(c, _):
        r0 = al(jnp.where(c == 0, first, lead + (c - 1) * block_rows), SMALL)
        rows = pl.ds(r0, block_rows)
        o0 = al(c * block_rows, block_rows)
        v = evaluate(r0, block_rows, ct_ref, ci_ref, cn_ref, 0, cols_pad)
        v = v - dot3(dot_nt, ph_ref[rows, :], pl_ref[rows, :],
                     ph_ref[cols0 : cols0 + cols_pad, :], pl_ref[cols0 : cols0 + cols_pad, :])
        if width is None:
            lead_out[pl.ds(o0, block_rows), :] = s_ref[rows, :]
            trail_out[pl.ds(o0, block_rows), :] = v
        else:
            q0 = al(pq_ref[1] * width, width)
            trail_out[pl.ds(o0, block_rows), 0:width] = s_ref[rows, pl.ds(q0, width)]
            trail_out[pl.ds(o0, block_rows), width:] = v
        return 0
    lax.fori_loop(0, groups, trailing, 0)


def per_device(replay_pool, sample_ids, rotation_bins):
    rows_n = lax.axis_size("row")
    cols_n = lax.axis_size("col")
    p = lax.axis_index("row")
    q = lax.axis_index("col")
    lead, feat = replay_pool.shape
    block_rows = lead // rows_n
    block_cols = lead // cols_n
    rows_other = (rows_n - 1) * block_rows
    cols_other = (rows_n - 1) * block_cols
    cols_pad = -(-cols_other // SMALL) * SMALL
    other = rows_other + cols_pad
    tile_other = max(t for t in range(SMALL, 513, SMALL) if other % t == 0)
    aligned = block_cols % SMALL == 0

    features = replay_pool[sample_ids[0]]
    bins = rotation_bins.astype(BF16)

    def trailer(values):
        flat = jnp.concatenate(values)
        return jnp.pad(flat, (0, 16 * feat - flat.shape[0])).reshape(16, feat)

    half = lead // 2
    h0 = (q % 2) * half
    message = jnp.concatenate(
        [lax.dynamic_slice_in_dim(features, h0, half, 0), trailer([lax.dynamic_slice_in_dim(bins, h0, half, 0)])])
    mine = jnp.where(p == 0, message, jnp.zeros_like(message))
    for d in range(1, rows_n):
        mine = mine + lax.ppermute(message, "row", [(0, d)])
    theirs = lax.ppermute(mine, "col", [(i, i ^ 1) for i in range(cols_n)])
    even = q % 2 == 0
    low, high = jnp.where(even, mine, theirs), jnp.where(even, theirs, mine)
    lead_feats = jnp.concatenate([low[:half], high[:half]])
    lead_bins = jnp.concatenate([low[half:].reshape(-1)[:half], high[half:].reshape(-1)[:half]])

    c0 = q * block_cols
    col_piece = lax.dynamic_slice_in_dim(features, c0, block_cols, 0)
    col_bins = lax.dynamic_slice_in_dim(bins, c0, block_cols, 0)
    out = jnp.concatenate([
        features.reshape(rows_n, block_rows, feat),
        jnp.broadcast_to(col_piece[None], (rows_n, block_cols, feat)),
        jnp.stack([trailer([bins[r * block_rows : (r + 1) * block_rows], col_bins]) for r in range(rows_n)]),
    ], axis=1)
    got = lax.all_to_all(out, "row", split_axis=0, concat_axis=0)
    row_feats = got[1:, :block_rows].reshape(rows_other, feat)
    col_feats = got[1:, block_rows : block_rows + block_cols].reshape(cols_other, feat)
    tails = got[1:, block_rows + block_cols :].reshape(rows_n - 1, -1)
    row_bins = tails[:, :block_rows].reshape(-1)
    col_bins = tails[:, block_rows : block_rows + block_cols].reshape(-1)
    groups = jnp.arange(1, rows_n, dtype=jnp.int32)[:, None] * lead
    row_ids = (groups + p * block_rows + jnp.arange(block_rows, dtype=jnp.int32)[None]).reshape(-1)
    col_ids = (groups + c0 + jnp.arange(block_cols, dtype=jnp.int32)[None]).reshape(-1)
    extra = cols_pad - cols_other
    col_feats = jnp.pad(col_feats, ((0, extra), (0, 0)))
    col_bins = jnp.pad(col_bins, (0, extra))
    col_ids = jnp.pad(col_ids, (0, extra), constant_values=-1)

    x = jnp.concatenate([lead_feats, row_feats, col_feats])
    angle = jnp.concatenate([lead_bins, row_bins, col_bins]).astype(F32) * (2.0 * np.pi / ROTS)
    ids = jnp.concatenate([jnp.arange(lead, dtype=jnp.int32), row_ids, col_ids]).astype(F32)
    info = jnp.stack([jnp.cos(angle), jnp.sin(angle), ids, jnp.zeros_like(ids)], axis=0)
    xi = info.T
    pad = jnp.zeros((4, info.shape[1]), F32)
    info = jnp.concatenate([info, pad])
    lt = lead_feats.T * BF16(1.0 / 256.0)
    ct = col_feats.T * BF16(1.0 / 256.0)
    lt = jnp.concatenate([lt, lt])
    ct = jnp.concatenate([ct, ct])
    pq = jnp.stack([p, q]).astype(jnp.int32)

    total = lead + other
    dims = (lead, other, block_rows, rows_other, tile_other, block_cols if aligned else None)
    own = rows_n * block_rows
    trail_width = cols_pad + (block_cols if aligned else 0)
    shapes = [jax.ShapeDtypeStruct((own, trail_width), F32)]
    if not aligned:
        shapes.append(jax.ShapeDtypeStruct((own, lead), F32))
    vmem = pl.BlockSpec(memory_space=pltpu.VMEM)
    tile, *lead_out = pl.pallas_call(
        functools.partial(mega_kernel, dims),
        out_shape=shapes,
        in_specs=[pl.BlockSpec(memory_space=pltpu.SMEM)] + [vmem] * 6,
        out_specs=[vmem] * len(shapes),
        scratch_shapes=[
            pltpu.VMEM((total, lead), F32),
            pltpu.VMEM((total, lead), BF16),
            pltpu.VMEM((total, lead), BF16),
            pltpu.VMEM((BIG, BIG), F32),
            pltpu.VMEM((BIG, BIG), F32),
            pltpu.VMEM((8, lead), F32),
            pltpu.VMEM((8, cols_pad), F32),
        ],
        compiler_params=pltpu.CompilerParams(vmem_limit_bytes=56 * 2**20),
        name="panel",
    )(pq, x, lt, ct, xi, info[:, :lead], info[:, lead + rows_other :])
    if aligned:
        return tile
    leading = lax.dynamic_slice_in_dim(lead_out[0], c0, block_cols, 1)
    return jnp.concatenate([leading, tile[:, :cols_other]], axis=1)


def solution(mesh):
    in_specs = (P("row", None), P("row", None), P("row"))
    return jax.shard_map(per_device, mesh=mesh, in_specs=in_specs, out_specs=P("row", "col"), check_vma=False)
```

```python
import functools

import jax
import jax.numpy as jnp
import numpy as np
from jax import lax
from jax.experimental import pallas as pl
from jax.experimental.pallas import tpu as pltpu
from jax.sharding import PartitionSpec as P

ROTS = 16
SHARPNESS = 2.0
RIDGE = 0.1
BIG = 256
SMALL = 128
TAIL = 16
VMEM_BYTES = 60 * 2**20
F32, BF16 = jnp.float32, jnp.bfloat16


def split(x):
    hi = x.astype(BF16)
    return hi, (x - hi.astype(F32)).astype(BF16)


def dot_nt(a, b):
    return lax.dot_general(a, b, (((1,), (1,)), ((), ())), preferred_element_type=F32)


def dot_nn(a, b):
    return jnp.dot(a, b, preferred_element_type=F32)


def dot3(dot, ah, al, bh, bl):
    return dot(ah, bh) + (dot(ah, bl) + dot(al, bh))


def gauss_jordan(rows):
    groups = len(rows)
    shape = (8, SMALL)
    sub = lax.broadcasted_iota(jnp.int32, shape, 0)
    lane = lax.broadcasted_iota(jnp.int32, shape, 1)
    left = list(rows)
    right = [jnp.where(sub + 8 * g == lane, 1.0, 0.0).astype(F32) for g in range(groups)]
    out = []
    for g in range(groups):
        a, b = left[g], right[g]
        cols = [jnp.broadcast_to(a[:, 8 * g + k : 8 * g + k + 1], shape) for k in range(8)]
        kept = jnp.zeros(shape, F32)
        for k in range(8):
            pivot = jnp.broadcast_to(cols[k][k : k + 1, :], shape)
            inv = 1.0 / pivot
            mult = jnp.where(sub == k, 1.0 - inv, cols[k] * inv)
            arow = jnp.broadcast_to(a[k : k + 1, :], shape)
            brow = jnp.broadcast_to(b[k : k + 1, :], shape)
            kept = jnp.where(sub == k, brow * lax.rsqrt(pivot), kept)
            a = a - mult * arow
            b = b - mult * brow
            for j in range(k + 1, 8):
                cols[j] = cols[j] - mult * jnp.broadcast_to(cols[j][k : k + 1, :], shape)
        out.append(kept)
        for i in range(g + 1, groups):
            suma = sumb = None
            for k in range(8):
                c = jnp.broadcast_to(left[i][:, 8 * g + k : 8 * g + k + 1], shape)
                ta = c * jnp.broadcast_to(a[k : k + 1, :], shape)
                tb = c * jnp.broadcast_to(b[k : k + 1, :], shape)
                suma, sumb = (ta, tb) if suma is None else (suma + ta, sumb + tb)
            left[i] = left[i] - suma
            right[i] = right[i] - sumb
    return out


def iota(n, axis):
    shape = (n, 1) if axis == 0 else (1, n)
    return lax.broadcasted_iota(jnp.int32, shape, axis)


def ridge(row_ids, col_ids):
    return jnp.where(row_ids == col_ids, RIDGE, 0.0).astype(F32)


def al(v, m):
    return pl.multiple_of(v, m)


def evaluate(acc_ref, x_ref, row0, tm, t_ref, li_ref, xi_ref, col0, tn):
    feat = x_ref.shape[1]
    chan = feat // ROTS
    acc = acc_ref.at[0:tm, 0:tn]
    for s in range(ROTS):
        w = t_ref[feat - chan * s : 2 * feat - chan * s, pl.ds(col0, tn)]
        e = jnp.exp(dot_nn(x_ref[pl.ds(row0, tm), :], w))
        acc[...] = e if s == 0 else acc[...] + e
    af = x_ref[pl.ds(row0, tm), :].astype(F32)
    rn = jnp.sum(af * af, axis=1, keepdims=True) * (1.0 / feat) + SHARPNESS
    info = xi_ref[pl.ds(row0, tm), :]
    cc, cs, cn = (li_ref[k : k + 1, pl.ds(col0, tn)] for k in range(3))
    arg = info[:, 0:1] * cc + info[:, 1:2] * cs - rn - cn
    return acc[...] * jnp.exp(arg) * (1.0 / ROTS)


def unpack_rows(block_rows, block_cols, q, got_ref, swap_ref, x_ref, b_ref, groups, row0):
    half = block_rows // 2
    tail = half + block_cols
    for n, c in enumerate(groups):
        at = row0 + n * block_rows
        mine, theirs = (al(at + ((q % 2) ^ k) * half, half) for k in range(2))
        x_ref[pl.ds(mine, half), :] = got_ref[c, 0:half, :]
        x_ref[pl.ds(theirs, half), :] = swap_ref[c, :, :]
        b_ref[0:1, at : at + block_rows] = got_ref[c, tail : tail + 1, 0:block_rows].astype(F32)


def unpack_cols(block_rows, block_cols, got_ref, x_ref, b_ref, row0):
    half = block_rows // 2
    tail = half + block_cols
    for n in range(got_ref.shape[0] - 1):
        at = row0 + n * block_cols
        x_ref[at : at + block_cols, :] = got_ref[n + 1, half:tail, :]
        bins = got_ref[n + 1, tail : tail + 1, block_rows : block_rows + block_cols]
        b_ref[0:1, at : at + block_cols] = bins.astype(F32)


def spread_info(x_ref, t_ref, b_ref, flip_ref, xi_ref, li_ref, col0, cols):
    feat = x_ref.shape[1]
    rows = x_ref.shape[0]
    bins = b_ref[0:1, :]
    cos, sin = jnp.zeros_like(bins), jnp.zeros_like(bins)
    for v in range(ROTS):
        hit = bins == float(v)
        cos = jnp.where(hit, float(np.cos(2.0 * np.pi * v / ROTS)), cos)
        sin = jnp.where(hit, float(np.sin(2.0 * np.pi * v / ROTS)), sin)
    flip_ref[0:1, :] = SHARPNESS * cos
    flip_ref[1:2, :] = SHARPNESS * sin
    for n in range(rows // SMALL):
        at = slice(n * SMALL, (n + 1) * SMALL)
        xi_ref[at, :] = flip_ref[:, at].T
    li_ref[0:1, :] = cos[:, col0 : col0 + cols]
    li_ref[1:2, :] = sin[:, col0 : col0 + cols]
    eye = jnp.where(iota(feat, 0) == iota(feat, 1), 1.0 / 256.0, 0.0).astype(BF16)
    for n in range(cols // SMALL):
        at = slice(n * SMALL, (n + 1) * SMALL)
        t = dot_nt(eye, x_ref[col0 + n * SMALL : col0 + (n + 1) * SMALL, :])
        li_ref[2:3, at] = jnp.sum(t * t, axis=0, keepdims=True) * (256.0 * 256.0 / feat)
        t = t.astype(BF16)
        t_ref[0:feat, at] = t
        t_ref[feat : 2 * feat, at] = t


def pack_kernel(pq_ref, pool_ref, ids_ref, bins_ref, col_bins_ref, out_ref, lead_ref, f_ref, flip_ref):
    q = pq_ref[1]
    lead, feat = pool_ref.shape
    groups, rows, _ = out_ref.shape
    block_rows = lead // groups
    half = block_rows // 2
    block_cols = rows - half - TAIL
    quarter = lead // 4
    flip_ref[0:1, :] = ids_ref[...].astype(F32)
    for n in range(lead // SMALL):
        at = slice(n * SMALL, (n + 1) * SMALL)
        ids = flip_ref[:, at].T[:, 0:1].astype(jnp.int32)
        hot = jnp.where(ids == iota(lead, 1), 1.0, 0.0).astype(BF16)
        f_ref[at, :] = dot_nn(hot, pool_ref[...]).astype(BF16)
    bins = bins_ref[...].astype(F32)
    flip_ref[0:1, :] = bins
    piece = f_ref[pl.ds(al(q * block_cols, block_cols), block_cols), :]
    for r in range(groups):
        out_ref[r, 0:half, :] = f_ref[pl.ds(al(r * block_rows + (q % 2) * half, half), half), :]
        out_ref[r, half : half + block_cols, :] = piece
        tail = jnp.concatenate(
            [bins[:, r * block_rows : (r + 1) * block_rows], col_bins_ref[...].astype(F32)], axis=1)
        tail = jnp.pad(tail, ((0, TAIL - 1), (0, feat - tail.shape[1])))
        out_ref[r, half + block_cols :, :] = tail.astype(BF16)
    at = pl.ds(al((q % 4) * quarter, quarter), quarter)
    lead_ref[0:quarter, :] = f_ref[at, :]
    tail = jnp.pad(flip_ref[0:1, at], ((0, TAIL - 1), (0, feat - quarter)))
    lead_ref[quarter:, :] = tail.astype(BF16)


def trail_kernel(block_rows, block_cols, lead, pq_ref, got_ref, swap_ref, out_ref, x_ref, t_ref, b_ref, flip_ref, xi_ref, li_ref, *acc_refs):
    p, q = pq_ref[0], pq_ref[1]
    groups = got_ref.shape[0]
    own = groups * block_rows
    cols = (groups - 1) * block_cols
    cols_pad = out_ref.shape[1]
    b_ref[...] = jnp.zeros(b_ref.shape, F32)
    unpack_rows(block_rows, block_cols, q, got_ref, swap_ref, x_ref, b_ref, range(groups), 0)
    unpack_cols(block_rows, block_cols, got_ref, x_ref, b_ref, own)
    if cols < cols_pad:
        x_ref[own + cols :, :] = jnp.zeros((cols_pad - cols, x_ref.shape[1]), BF16)
    spread_info(x_ref, t_ref, b_ref, flip_ref, xi_ref, li_ref, own, cols_pad)
    lane = iota(cols_pad, 1)
    col_ids = (lane // block_cols + 1) * lead + q * block_cols + lane % block_cols

    def tile(n, _):
        for u in range(len(acc_refs)):
            c = n * len(acc_refs) + u
            row0 = al(c * block_rows, block_rows)
            v = evaluate(acc_refs[u], x_ref, row0, block_rows, t_ref, li_ref, xi_ref, 0, cols_pad)
            row_ids = c * lead + p * block_rows + iota(block_rows, 0)
            out_ref[pl.ds(row0, block_rows), :] = v + ridge(row_ids, col_ids)
        return 0
    lax.fori_loop(0, groups // len(acc_refs), tile, 0)


def panel_kernel(dims, jobs_ref, pq_ref, q0_ref, q1_ref, q2_ref, q3_ref, got_ref, swap_ref, k_ref, trail_out, *refs):
    lead, other, block_rows, block_cols, tile_other = dims
    width = block_cols if block_cols % SMALL == 0 else None
    if width is None:
        lead_out, *refs = refs
    s_ref, ph_ref, pl_ref, d_ref, x32_ref, x_ref, lt_ref, b_ref, flip_ref, xi_ref, li_ref, *acc_refs = refs
    feat = x_ref.shape[1]
    nbig = lead // BIG
    others = other // tile_other
    groups = got_ref.shape[0]
    half = block_rows // 2
    rows_other = (groups - 1) * block_rows
    cols_pad = other - rows_other
    p, q = pq_ref[0], pq_ref[1]

    first = al(p * block_rows, block_rows)

    def lead_tile(acc_ref, row0, col0, scale=None):
        v = evaluate(acc_ref, x_ref, row0, BIG, lt_ref, li_ref, xi_ref, col0, BIG)
        v = v + ridge(row0 + iota(BIG, 0), col0 + iota(BIG, 1))
        at = (pl.ds(row0, BIG), pl.ds(col0, BIG))
        s_ref[at] = s_ref[at] + (v if scale is None else v * scale)

    def lead_job(acc_ref, n):
        row0, col0 = al(jobs_ref[3 * n], BIG), al(jobs_ref[3 * n + 1], BIG)
        lead_tile(acc_ref, row0, col0, jobs_ref[3 * n + 2].astype(F32))

    def other_tile(acc_ref, i, j):
        row0, col0 = lead + i * tile_other, al(j * BIG, BIG)
        at = (pl.ds(row0, tile_other), pl.ds(col0, BIG))
        s_ref[at] = s_ref[at] + evaluate(
            acc_ref, x_ref, row0, tile_other, lt_ref, li_ref, xi_ref, col0, BIG)

    def own_row(c):
        return al(jnp.where(c == 0, first, lead + (c - 1) * block_rows), SMALL)

    left = 0 if width is None else width

    quarter = lead // 4
    b_ref[...] = jnp.zeros(b_ref.shape, F32)
    for ref, flip in ((q0_ref, 0), (q1_ref, 1), (q2_ref, 2), (q3_ref, 3)):
        at = al(((q % 4) ^ flip) * quarter, quarter)
        x_ref[pl.ds(at, quarter), :] = ref[0:quarter, :]
        b_ref[0:1, pl.ds(at, quarter)] = ref[quarter : quarter + 1, 0:quarter].astype(F32)
    unpack_rows(block_rows, block_cols, q, got_ref, swap_ref, x_ref, b_ref, range(1, groups), lead)
    unpack_cols(block_rows, block_cols, got_ref, x_ref, b_ref, lead + rows_other)
    if (groups - 1) * block_cols < cols_pad:
        at = lead + rows_other + (groups - 1) * block_cols
        x_ref[at:, :] = jnp.zeros((lead + other - at, feat), BF16)
    spread_info(x_ref, lt_ref, b_ref, flip_ref, xi_ref, li_ref, 0, lead)

    def clear(i, _):
        at = pl.ds(al(i * SMALL, SMALL), SMALL)
        s_ref[at, :] = jnp.zeros((SMALL, lead), F32)
        ph_ref[at, :] = jnp.zeros((SMALL, lead), BF16)
        pl_ref[at, :] = jnp.zeros((SMALL, lead), BF16)
        return 0
    lax.fori_loop(0, (lead + other) // SMALL, clear, 0)
    lead_tile(acc_refs[0], 0, 0)
    lead_tile(acc_refs[1], BIG, 0)

    def invert(r0):
        rows = [d_ref[r0 + 8 * g : r0 + 8 * g + 8, r0 : r0 + SMALL] for g in range(SMALL // 8)]
        for g, v in enumerate(gauss_jordan(rows)):
            x32_ref[r0 + 8 * g : r0 + 8 * g + 8, r0 : r0 + SMALL] = v

    def big_step(j, last):
        c0 = al(j * BIG, BIG)
        cj = pl.ds(c0, BIG)
        work = [functools.partial(other_tile, i=i, j=j) for i in range(others)]
        if not last:
            work[others - 1 : others - 1] = [
                functools.partial(lead_job, n=j * (nbig - 1) + u) for u in range(nbig - 1)]
        cut = -(-len(work) // 2)
        d_ref[...] = s_ref[cj, cj]
        invert(0)
        for n, job in enumerate(work[:cut]):
            job(acc_refs[n % len(acc_refs)])
        x11 = split(x32_ref[0:SMALL, 0:SMALL])
        l21 = split(dot3(dot_nt, *split(d_ref[SMALL:, 0:SMALL]), *x11))
        d_ref[SMALL:, SMALL:] = d_ref[SMALL:, SMALL:] - dot3(dot_nt, *l21, *l21)
        invert(SMALL)
        mid = split(dot3(dot_nn, *l21, *x11))
        for n, job in enumerate(work[cut:]):
            job(acc_refs[n % len(acc_refs)])
        x22 = split(x32_ref[SMALL:, SMALL:])
        x32_ref[SMALL:, 0:SMALL] = -dot3(dot_nn, *x22, *mid)
        x32_ref[0:SMALL, SMALL:] = jnp.zeros((SMALL, SMALL), F32)
        xh, xl = split(x32_ref[...])

        def solve(r0, tm, mask):
            v = dot3(dot_nt, *split(s_ref[pl.ds(r0, tm), cj]), xh, xl)
            if mask:
                keep = lax.broadcasted_iota(jnp.int32, v.shape, 0) >= lax.broadcasted_iota(jnp.int32, v.shape, 1)
                v = jnp.where(keep, v, 0.0)
            s_ref[pl.ds(r0, tm), cj] = v
            h, l = split(v)
            ph_ref[pl.ds(r0, tm), cj] = h
            pl_ref[pl.ds(r0, tm), cj] = l

        solve(c0, BIG, True)
        if not last:
            def lead_solve(i, _):
                solve(al(i * BIG, BIG), BIG, False)
                return 0
            lax.fori_loop(j + 1, nbig, lead_solve, 0)
        def other_solve(i, _):
            solve(al(lead + i * tile_other, SMALL), tile_other, False)
            return 0
        lax.fori_loop(0, others, other_solve, 0)
        if last:
            return

        def update(r0, tm, k0):
            kj = pl.ds(k0, BIG)
            rows = pl.ds(r0, tm)
            s_ref[rows, kj] = s_ref[rows, kj] - dot3(
                dot_nt, ph_ref[rows, cj], pl_ref[rows, cj], ph_ref[kj, cj], pl_ref[kj, cj])

        def update_col(k, _):
            k0 = al(k * BIG, BIG)
            def lead_update(i, _):
                update(al(i * BIG, BIG), BIG, k0)
                return 0
            lax.fori_loop(k, nbig, lead_update, 0)
            def other_update(i, _):
                update(al(lead + i * tile_other, SMALL), tile_other, k0)
                return 0
            lax.fori_loop(0, others, other_update, 0)
            return 0
        lax.fori_loop(j + 1, nbig, update_col, 0)

    def loop_step(j, _):
        big_step(j, False)
        return 0
    lax.fori_loop(0, nbig - 1, loop_step, 0)
    big_step(nbig - 1, True)

    cols0 = lead + rows_other

    def trailing(c, _):
        rows = pl.ds(own_row(c), block_rows)
        at = pl.ds(al(c * block_rows, block_rows), block_rows)
        trail_out[at, left:] = k_ref[at, :] - dot3(
            dot_nt, ph_ref[rows, :], pl_ref[rows, :],
            ph_ref[cols0 : cols0 + cols_pad, :], pl_ref[cols0 : cols0 + cols_pad, :])
        if width is None:
            lead_out[at, :] = s_ref[rows, :]
        else:
            trail_out[at, 0:width] = s_ref[rows, pl.ds(al(q * width, width), width)]
        return 0
    lax.fori_loop(0, groups, trailing, 0)


def job_table(nbig):
    table = []
    for t in range(nbig - 1):
        tiles = [(i, t) for i in range(t + 1, nbig)] + [(t + 1, t + 1)]
        tiles = tiles[1:] if t == 0 else tiles
        tiles = [(i * BIG, j * BIG, 1) for i, j in tiles]
        table += tiles + [(0, 0, 0)] * (nbig - 1 - len(tiles))
    return np.array(table, np.int32).reshape(-1)


def per_device(replay_pool, sample_ids, rotation_bins):
    rows_n = lax.axis_size("row")
    cols_n = lax.axis_size("col")
    p = lax.axis_index("row")
    q = lax.axis_index("col")
    lead, feat = replay_pool.shape
    block_rows = lead // rows_n
    block_cols = lead // cols_n
    rows_other = (rows_n - 1) * block_rows
    cols_other = (rows_n - 1) * block_cols
    cols_pad = -(-cols_other // SMALL) * SMALL
    other = rows_other + cols_pad
    total = lead + other
    own = rows_n * block_rows
    half = block_rows // 2
    tile_other = max(t for t in range(SMALL, 513, SMALL) if other % t == 0)
    aligned = block_cols % SMALL == 0
    smem = pl.BlockSpec(memory_space=pltpu.SMEM)
    vmem = pl.BlockSpec(memory_space=pltpu.VMEM)
    params = pltpu.CompilerParams(vmem_limit_bytes=VMEM_BYTES)
    pq = jnp.stack([p, q]).astype(jnp.int32)

    def shape(*dims, dtype=F32):
        return jax.ShapeDtypeStruct(dims, dtype)

    message, quarter = pl.pallas_call(
        pack_kernel,
        out_shape=(shape(rows_n, half + block_cols + TAIL, feat, dtype=BF16), shape(lead // 4 + TAIL, feat, dtype=BF16)),
        in_specs=[smem] + [vmem] * 4,
        out_specs=(vmem, vmem),
        scratch_shapes=[pltpu.VMEM((lead, feat), BF16), pltpu.VMEM((SMALL, lead), F32)],
        compiler_params=params,
        name="pack",
    )(pq, replay_pool, sample_ids, rotation_bins[None],
      lax.dynamic_slice_in_dim(rotation_bins, q * block_cols, block_cols, 0)[None])

    got = lax.all_to_all(message, "row", split_axis=0, concat_axis=0)
    swap = lax.ppermute(got[:, :half], "col", [(i, i ^ 1) for i in range(cols_n)])

    mine = jnp.where(p == 0, quarter, jnp.zeros_like(quarter))
    for d in range(1, rows_n):
        mine = mine + lax.ppermute(quarter, "row", [(0, d)])
    over_z = lax.ppermute(mine, "col", [(i, i ^ 2) for i in range(cols_n)])
    sibling = lax.ppermute(mine, "col", [(i, i ^ 1) for i in range(cols_n)])
    both = lax.ppermute(over_z, "col", [(i, i ^ 1) for i in range(cols_n)])

    trailing = pl.pallas_call(
        functools.partial(trail_kernel, block_rows, block_cols, lead),
        out_shape=shape(own, cols_pad),
        in_specs=[smem] + [vmem] * 2,
        out_specs=vmem,
        scratch_shapes=[
            pltpu.VMEM((own + cols_pad, feat), BF16),
            pltpu.VMEM((2 * feat, cols_pad), BF16),
            pltpu.VMEM((8, own + cols_pad), F32),
            pltpu.VMEM((SMALL, own + cols_pad), F32),
            pltpu.VMEM((own + cols_pad, SMALL), F32),
            pltpu.VMEM((8, cols_pad), F32),
        ] + [pltpu.VMEM((block_rows, cols_pad), F32)] * 2,
        compiler_params=params,
        cost_estimate=pl.CostEstimate(
            flops=2 * ROTS * own * cols_pad * feat, bytes_accessed=8 * own * cols_pad, transcendentals=0),
        name="trail",
    )(pq, got, swap)

    shapes = [shape(own, cols_pad + (block_cols if aligned else 0))]
    if not aligned:
        shapes.append(shape(own, lead))
    tile, *lead_out = pl.pallas_call(
        functools.partial(panel_kernel, (lead, other, block_rows, block_cols, tile_other)),
        out_shape=shapes,
        in_specs=[smem] * 2 + [vmem] * 7,
        out_specs=[vmem] * len(shapes),
        scratch_shapes=[
            pltpu.VMEM((total, lead), F32),
            pltpu.VMEM((total, lead), BF16),
            pltpu.VMEM((total, lead), BF16),
            pltpu.VMEM((BIG, BIG), F32),
            pltpu.VMEM((BIG, BIG), F32),
            pltpu.VMEM((total, feat), BF16),
            pltpu.VMEM((2 * feat, lead), BF16),
            pltpu.VMEM((8, total), F32),
            pltpu.VMEM((SMALL, total), F32),
            pltpu.VMEM((total, SMALL), F32),
            pltpu.VMEM((8, lead), F32),
        ] + [pltpu.VMEM((max(BIG, tile_other), BIG), F32)] * 4,
        compiler_params=params,
        name="panel",
    )(jnp.asarray(job_table(lead // BIG)), pq, mine, sibling, over_z, both, got, swap, trailing)
    if aligned:
        return tile
    leading = lax.dynamic_slice_in_dim(lead_out[0], q * block_cols, block_cols, 1)
    return jnp.concatenate([leading, tile[:, :cols_other]], axis=1)


def solution(mesh):
    in_specs = (P("row", None), P("row", None), P("row"))
    return jax.shard_map(per_device, mesh=mesh, in_specs=in_specs, out_specs=P("row", "col"), check_vma=False)
```
